32 devices in a mesh: dp: 4 (over y, x), hidden: 8 (over z, core).
Axes of the slice: x: 2, y: 2, z: 4, core: 2. Of those that a mesh axis runs over, the one named last changes fastest.
Arguments:
- tokens: bfloat16 [2048, 6144], P('dp', 'hidden'), as said below
- cotangent: bfloat16 [2048, 6144], P('dp', 'hidden'), may hold values from -6 to 6
- weight_in: bfloat16 [6144, 3072], P('hidden'), may hold values from -0.21875 to 0.21875
- level_weights: bfloat16 [3, 192, 2, 128, 128], P(None, 'hidden'), may hold values from -0.375 to 0.375
- weight_out: bfloat16 [24576, 768], P('hidden'), may hold values from -0.109375 to 0.109375
- block_order: int32 [3, 24], replicated, may hold values from 0 to 23, each once within a row
Outputs:
- branch_output: bfloat16 [2048, 6144], P('dp', 'hidden')
- token_grad: bfloat16 [2048, 6144], P('dp', 'hidden')
- level_grad: float32 [3, 192, 2, 128, 128], P(None, 'hidden', None, 'dp')
- input_grad: float32 [6144, 3072], P(('hidden', 'dp'))
- output_grad: float32 [24576, 768], P(('hidden', 'dp'))
The draws below stay inside these ranges and needn't reach their ends.
Inputs may be any that keep to these rules, and one draw needn't show every extreme that they name: Each row of block_order lists every number from 0 to 23 once. `tokens`: entries are finite.
All inputs are finite; a program needn't handle non-finite values.
Results may differ from the reference program's by a relative error of at most 0.017.
Values may be sent and summed in bfloat16 or wider, within the bound.
A program may use at most 192 MiB of HBM per device.

```python
import math
import jax
import jax.numpy as jnp
from jax import lax

D = 6144
FF = 24576
BLK = 128
TOK_DEV = 512
LEVELS = 3
BF = 24
NBF = 192
TOKENS = 2048
N_DP = 4
N_HIDDEN = 8


def draw_tokens(key, part):
    first, second, third = jax.random.split(key, 3)
    column = jnp.arange(D, dtype=jnp.float32) / D
    base = jax.random.normal(first, (TOKENS, D), jnp.float32)
    rising = jnp.exp(column * math.log(3.0))
    column_scale = rising * jnp.exp(jax.random.uniform(second, (D,), jnp.float32, 0.0, math.log(4.0)))
    row_scale = jnp.exp(jax.random.uniform(third, (TOKENS, 1), jnp.float32, 0.0, math.log(10.0)))
    return (base * column_scale * row_scale).astype(jnp.bfloat16)


def block_levels(rng, shape, cuts, smallest, high):
    def one(axis_at, parts):
        heights = jax.random.uniform(jax.random.fold_in(jax.random.fold_in(rng, 6), axis_at), (parts,), jnp.float32, smallest / len(cuts), high / len(cuts))
        return jnp.repeat(jnp.exp(heights), shape[axis_at] // parts).reshape((-1,) + (1,) * (len(shape) - axis_at - 1))

    gain = one(*cuts[0])
    for cut in cuts[1:]:
        gain = gain * one(*cut)
    return gain


def normal_values(stream_key, shape, spread, most, shards=(), kind=jnp.bfloat16):
    result = spread * jax.random.normal(stream_key, shape, jnp.float32)
    if shards:
        result = result * block_levels(stream_key, shape, shards, -0.22, 0.18)
    return jnp.clip(result, -most, most).astype(kind)


def setup_inputs(seed: int = 0) -> dict:
    seeds = jax.random.split(jax.random.key(seed), 7)
    return {
        "tokens": draw_tokens(jax.random.fold_in(seeds[6], 71), 0),
        "cotangent": normal_values(seeds[1], (TOKENS, D), 1.0, 6.0, ((0, 4), (1, 8))),
        "weight_in": normal_values(seeds[2], (D, FF // N_HIDDEN), (D // N_HIDDEN) ** -0.5, 0.21875, ((0, 8),)),
        "level_weights": normal_values(seeds[3], (LEVELS, NBF, 2, BLK, BLK), (2 * BLK) ** -0.5, 0.375, ((1, 8),)),
        "weight_out": normal_values(seeds[4], (FF, D // N_HIDDEN), (FF // N_HIDDEN) ** -0.5, 0.109375, ((0, 8),)),
        "block_order": jax.vmap(lambda own: jax.random.permutation(own, BF))(jax.random.split(seeds[5], LEVELS)).reshape((LEVELS, BF)).astype(jnp.int32),
    }


def flip_pairs(values, level_index):
    shape = values.shape
    split = values.reshape(shape[0], shape[1] >> level_index + 1, 2, 1 << level_index, shape[2], shape[3])
    return split[:, :, ::-1].reshape(shape)

def reference(tokens, cotangent, weight_in, level_weights, weight_out, block_order):
    wide = jnp.float32
    groups = N_HIDDEN
    width_local = D // N_HIDDEN
    units_local = FF // N_HIDDEN
    weights_first = weight_in.astype(wide).reshape(groups, width_local, units_local)
    weights_last = weight_out.astype(wide).reshape(groups, units_local, width_local)
    butterfly = level_weights.astype(wide).reshape(LEVELS, groups, BF, 2, BLK, BLK)
    positions = jnp.broadcast_to(jnp.arange(BF, dtype=jnp.int32), (LEVELS, BF))
    inverse = jnp.zeros_like(block_order).at[jnp.arange(LEVELS)[:, None], block_order].set(positions)
    grad_scale = 1.0 / math.sqrt(TOKENS)

    def one_block(carry, pieces):
        level_acc, first_acc, last_acc = carry
        tok_block, cot_block = pieces
        row_count = tok_block.shape[0]
        tokens_wide = tok_block.astype(wide)
        recip_rms = lax.rsqrt(lax.optimization_barrier(jnp.mean(tokens_wide * tokens_wide, axis=1, keepdims=True)) + 1e-06)
        normed = (tokens_wide * recip_rms).astype(jnp.bfloat16)
        normed_groups = normed.astype(wide).reshape(row_count, groups, width_local)
        current = jnp.einsum('rpc,pcf->rpf', normed_groups, weights_first).astype(jnp.bfloat16)
        current = current.reshape(row_count, groups, BF, BLK)
        inputs_kept = []
        partner_kept = []
        for level_index in range(LEVELS):
            shifted = flip_pairs(current, level_index)[:, :, block_order[level_index]]
            mixed_out = jnp.einsum('rpjc,pjcd->rpjd', current.astype(wide), butterfly[level_index, :, :, 0])
            mixed_out = mixed_out + jnp.einsum('rpjc,pjcd->rpjd', shifted.astype(wide), butterfly[level_index, :, :, 1])
            inputs_kept.append(current)
            partner_kept.append(shifted)
            current = mixed_out.astype(jnp.bfloat16)
        top_layer = current.astype(wide).reshape(row_count, groups, units_local)
        activated = jax.nn.gelu(top_layer).astype(jnp.bfloat16).astype(wide)
        result_out = jnp.einsum('rpf,pfd->rpd', activated, weights_last).astype(jnp.bfloat16)
        cot_groups = cot_block.astype(wide).reshape(row_count, groups, width_local)
        last_grad = jnp.einsum('rpf,rpd->pfd', activated, cot_groups) * grad_scale
        d_hidden = jnp.einsum('rpd,pfd->rpf', cot_groups, weights_last)
        _, pullback = jax.vjp(jax.nn.gelu, top_layer)
        upstream = pullback(d_hidden)[0].astype(jnp.bfloat16).reshape(row_count, groups, BF, BLK)
        level_list = [None] * LEVELS
        for level_index in reversed(range(LEVELS)):
            upstream_wide = upstream.astype(wide)
            grad_own = jnp.einsum('rpjc,rpjd->pjcd', inputs_kept[level_index].astype(wide), upstream_wide)
            grad_partner = jnp.einsum('rpjc,rpjd->pjcd', partner_kept[level_index].astype(wide), upstream_wide)
            level_list[level_index] = jnp.stack([grad_own, grad_partner], axis=2) * grad_scale
            own_term = jnp.einsum('rpjd,pjcd->rpjc', upstream_wide, butterfly[level_index, :, :, 0])
            sent_term = jnp.einsum('rpjd,pjcd->rpjc', upstream_wide, butterfly[level_index, :, :, 1]).astype(jnp.bfloat16)
            placed = flip_pairs(sent_term, level_index)[:, :, inverse[level_index]]
            upstream = (own_term + placed.astype(wide)).astype(jnp.bfloat16)
        flat_grad = upstream.astype(wide).reshape(row_count, groups, units_local)
        first_grad = jnp.einsum('rpc,rpf->pcf', normed_groups, flat_grad) * grad_scale
        d_normed = jnp.einsum('rpf,pcf->rpc', flat_grad, weights_first).reshape(row_count, D)
        inner_mean = lax.optimization_barrier(jnp.mean(d_normed * tokens_wide, axis=1, keepdims=True))
        token_out = (recip_rms * d_normed - tokens_wide * recip_rms * recip_rms * recip_rms * inner_mean).astype(jnp.bfloat16)
        new_carry = (level_acc + jnp.stack(level_list), first_acc + first_grad, last_acc + last_grad)
        return (new_carry, (result_out.reshape(row_count, D), token_out))
    start = (jnp.zeros((LEVELS, groups, BF, 2, BLK, BLK), wide), jnp.zeros((groups, width_local, units_local), wide), jnp.zeros((groups, units_local, width_local), wide))
    pieces = (tokens.reshape(N_DP, TOK_DEV, D), cotangent.reshape(N_DP, TOK_DEV, D))
    totals, outputs = lax.scan(one_block, start, pieces)
    branch_output = outputs[0].reshape(TOKENS, D)
    token_grad = outputs[1].reshape(TOKENS, D)
    level_grad = totals[0].reshape(LEVELS, NBF, 2, BLK, BLK)
    input_grad = totals[1].reshape(D, units_local)
    output_grad = totals[2].reshape(FF, width_local)
    return (branch_output, token_grad, level_grad, input_grad, output_grad)
```

```python
import math

import jax
import jax.numpy as jnp
from jax import lax
from jax.sharding import PartitionSpec as P


def partner(value, axis, distance):
    mask = 2**distance
    pairs = [(source, source ^ mask) for source in range(lax.axis_size(axis))]
    return lax.ppermute(value, axis, pairs)


def reduce_dp(value, dim, scale):
    summed = lax.psum_scatter(value.astype(jnp.bfloat16), "dp", scatter_dimension=dim, tiled=True)
    return summed.astype(jnp.float32) * scale


def local(tokens, cotangent, weight_in, level_weights, weight_out, block_order):
    wide = jnp.float32
    row_count, width_local = tokens.shape
    level_count, group_count = block_order.shape
    block_size = level_weights.shape[-1]
    feature_total = width_local * lax.axis_size("hidden")
    grad_scale = 1.0 / math.sqrt(row_count * lax.axis_size("dp"))
    tokens_wide = tokens.astype(wide)
    sum_squares = lax.psum(jnp.sum(tokens_wide * tokens_wide, axis=1), "hidden")
    recip_rms = lax.rsqrt(sum_squares / feature_total + 1e-06)[:, None]
    normed = (tokens_wide * recip_rms).astype(jnp.bfloat16)
    current = jnp.dot(normed, weight_in, preferred_element_type=wide).astype(jnp.bfloat16)
    current = current.reshape(row_count, group_count, block_size)
    positions = jnp.broadcast_to(
        jnp.arange(group_count, dtype=jnp.int32), (level_count, group_count)
    )
    inverse = (
        jnp.zeros_like(block_order).at[jnp.arange(level_count)[:, None], block_order].set(positions)
    )
    inputs_kept = []
    partner_kept = []
    for level_index in range(level_count):
        weights_now = level_weights[level_index]
        arrived = partner(current, "hidden", level_index)
        shifted = jnp.take(arrived, block_order[level_index], axis=1)
        mixed_out = jnp.einsum(
            "rjc,jcd->rjd", current, weights_now[:, 0], preferred_element_type=wide
        )
        mixed_out = mixed_out + jnp.einsum(
            "rjc,jcd->rjd", shifted, weights_now[:, 1], preferred_element_type=wide
        )
        inputs_kept.append(current)
        partner_kept.append(shifted)
        current = mixed_out.astype(jnp.bfloat16)
    top_layer = current.reshape(row_count, group_count * block_size).astype(wide)
    activated = jax.nn.gelu(top_layer).astype(jnp.bfloat16)
    result_out = jnp.dot(activated, weight_out, preferred_element_type=wide).astype(jnp.bfloat16)
    last_grad = reduce_dp(
        jnp.einsum("rf,rd->fd", activated, cotangent, preferred_element_type=wide), 0, grad_scale
    )
    d_hidden = jnp.einsum("rd,fd->rf", cotangent, weight_out, preferred_element_type=wide)
    _, pullback = jax.vjp(jax.nn.gelu, top_layer)
    upstream = (
        pullback(d_hidden)[0].astype(jnp.bfloat16).reshape(row_count, group_count, block_size)
    )
    level_list = [None] * level_count
    for level_index in reversed(range(level_count)):
        weights_now = level_weights[level_index]
        shifted = partner_kept[level_index]
        grad_own = jnp.einsum(
            "rjc,rjd->jcd", inputs_kept[level_index], upstream, preferred_element_type=wide
        )
        grad_partner = jnp.einsum("rjc,rjd->jcd", shifted, upstream, preferred_element_type=wide)
        stacked = jnp.stack([grad_own, grad_partner], axis=1)
        level_list[level_index] = reduce_dp(stacked, 2, grad_scale)
        own_term = jnp.einsum(
            "rjd,jcd->rjc", upstream, weights_now[:, 0], preferred_element_type=wide
        )
        sent_term = jnp.einsum(
            "rjd,jcd->rjc", upstream, weights_now[:, 1], preferred_element_type=wide
        ).astype(jnp.bfloat16)
        returned = partner(sent_term, "hidden", level_index)
        placed = jnp.take(returned, inverse[level_index], axis=1)
        upstream = (own_term + placed.astype(wide)).astype(jnp.bfloat16)
    flat_grad = upstream.reshape(row_count, group_count * block_size)
    first_grad = reduce_dp(
        jnp.einsum("rc,rf->cf", normed, flat_grad, preferred_element_type=wide), 0, grad_scale
    )
    d_normed = jnp.einsum("rf,cf->rc", flat_grad, weight_in, preferred_element_type=wide)
    inner_sum = lax.psum(jnp.sum(d_normed * tokens_wide, axis=1), "hidden")
    inner_mean = (inner_sum / feature_total)[:, None]
    token_out = (
        recip_rms * d_normed - tokens_wide * recip_rms * recip_rms * recip_rms * inner_mean
    ).astype(jnp.bfloat16)
    level_stack = jnp.stack(level_list)
    return (result_out, token_out, level_stack, first_grad, last_grad)


def solution(mesh):
    in_specs = (
        P("dp", "hidden"),
        P("dp", "hidden"),
        P("hidden", None),
        P(None, "hidden", None, None, None),
        P("hidden", None),
        P(),
    )
    out_specs = (
        P("dp", "hidden"),
        P("dp", "hidden"),
        P(None, "hidden", None, "dp", None),
        P(("hidden", "dp"), None),
        P(("hidden", "dp"), None),
    )
    return jax.shard_map(local, mesh=mesh, in_specs=in_specs, out_specs=out_specs, check_vma=False)
```

```python
import math

import jax
import jax.numpy as jnp
from jax import lax
from jax.sharding import PartitionSpec as P


def partner(value, axis, distance):
    mask = 2**distance
    pairs = [(source, source ^ mask) for source in range(lax.axis_size(axis))]
    return lax.ppermute(value, axis, pairs)


def reduce_dp(value, dim, scale):
    summed = lax.psum_scatter(value.astype(jnp.bfloat16), "dp", scatter_dimension=dim, tiled=True)
    return summed.astype(jnp.float32) * scale


def local(tokens, cotangent, weight_in, level_weights, weight_out, block_order):
    wide = jnp.float32
    row_count, width_local = tokens.shape
    level_count, group_count = block_order.shape
    block_size = level_weights.shape[-1]
    feature_total = width_local * lax.axis_size("hidden")
    grad_scale = 1.0 / math.sqrt(row_count * lax.axis_size("dp"))
    tokens_wide = tokens.astype(wide)
    sum_squares = lax.psum(jnp.sum(tokens_wide * tokens_wide, axis=1), "hidden")
    recip_rms = lax.rsqrt(sum_squares / feature_total + 1e-06)[:, None]
    normed = (tokens_wide * recip_rms).astype(jnp.bfloat16)
    current = jnp.dot(normed, weight_in, preferred_element_type=wide).astype(jnp.bfloat16)
    current = current.reshape(row_count, group_count, block_size)
    positions = jnp.broadcast_to(
        jnp.arange(group_count, dtype=jnp.int32), (level_count, group_count)
    )
    inverse = (
        jnp.zeros_like(block_order).at[jnp.arange(level_count)[:, None], block_order].set(positions)
    )
    inputs_kept = []
    partner_kept = []
    for level_index in range(level_count):
        weights_now = level_weights[level_index]
        arrived = partner(current, "hidden", level_index)
        shifted = jnp.take(arrived, block_order[level_index], axis=1)
        mixed_out = jnp.einsum(
            "rjc,jcd->rjd", current, weights_now[:, 0], preferred_element_type=wide
        )
        mixed_out = mixed_out + jnp.einsum(
            "rjc,jcd->rjd", shifted, weights_now[:, 1], preferred_element_type=wide
        )
        inputs_kept.append(current)
        partner_kept.append(shifted)
        current = mixed_out.astype(jnp.bfloat16)
    top_layer = current.reshape(row_count, group_count * block_size).astype(wide)
    activated = jax.nn.gelu(top_layer).astype(jnp.bfloat16)
    result_out = jnp.dot(activated, weight_out, preferred_element_type=wide).astype(jnp.bfloat16)
    last_grad = reduce_dp(
        jnp.einsum("rf,rd->fd", activated, cotangent, preferred_element_type=wide), 0, grad_scale
    )
    d_hidden = jnp.einsum("rd,fd->rf", cotangent, weight_out, preferred_element_type=wide)
    _, pullback = jax.vjp(jax.nn.gelu, top_layer)
    upstream = (
        pullback(d_hidden)[0].astype(jnp.bfloat16).reshape(row_count, group_count, block_size)
    )
    level_list = [None] * level_count
    for level_index in reversed(range(level_count)):
        weights_now = level_weights[level_index]
        sent_term = jnp.einsum(
            "rjd,jcd->rjc", upstream, weights_now[:, 1], preferred_element_type=wide
        ).astype(jnp.bfloat16)
        returned = partner(sent_term, "hidden", level_index)
        sent_term, upstream = lax.optimization_barrier((sent_term, upstream))
        shifted = partner_kept[level_index]
        grad_own = jnp.einsum(
            "rjc,rjd->jcd", inputs_kept[level_index], upstream, preferred_element_type=wide
        )
        grad_partner = jnp.einsum("rjc,rjd->jcd", shifted, upstream, preferred_element_type=wide)
        stacked = jnp.stack([grad_own, grad_partner], axis=1)
        level_list[level_index] = reduce_dp(stacked, 2, grad_scale)
        own_term = jnp.einsum(
            "rjd,jcd->rjc", upstream, weights_now[:, 0], preferred_element_type=wide
        )
        placed = jnp.take(returned, inverse[level_index], axis=1)
        upstream = (own_term + placed.astype(wide)).astype(jnp.bfloat16)
    flat_grad = upstream.reshape(row_count, group_count * block_size)
    first_grad = reduce_dp(
        jnp.einsum("rc,rf->cf", normed, flat_grad, preferred_element_type=wide), 0, grad_scale
    )
    d_normed = jnp.einsum("rf,cf->rc", flat_grad, weight_in, preferred_element_type=wide)
    inner_sum = lax.psum(jnp.sum(d_normed * tokens_wide, axis=1), "hidden")
    inner_mean = (inner_sum / feature_total)[:, None]
    token_out = (
        recip_rms * d_normed - tokens_wide * recip_rms * recip_rms * recip_rms * inner_mean
    ).astype(jnp.bfloat16)
    level_stack = jnp.stack(level_list)
    return (result_out, token_out, level_stack, first_grad, last_grad)


def solution(mesh):
    in_specs = (
        P("dp", "hidden"),
        P("dp", "hidden"),
        P("hidden", None),
        P(None, "hidden", None, None, None),
        P("hidden", None),
        P(),
    )
    out_specs = (
        P("dp", "hidden"),
        P("dp", "hidden"),
        P(None, "hidden", None, "dp", None),
        P(("hidden", "dp"), None),
        P(("hidden", "dp"), None),
    )
    return jax.shard_map(local, mesh=mesh, in_specs=in_specs, out_specs=out_specs, check_vma=False)
```
